256 devices in a mesh: cam: 128 (over z, x, y_lo, core), depth: 2 (over y_hi).
Axes of the slice: x: 4, y: 4 (y_hi: 2, y_lo: 2; y = y_hi * 2 + y_lo), z: 8, core: 2. Of those that a mesh axis runs over, the one named last changes fastest.
Arguments:
- features: bfloat16 [128, 32, 8, 512], P('cam'), may hold values from -6 to 6
- view_mask: int32 [128, 4], P('cam'), may hold values 0 or 1
- row_offset: int32 [128, 4, 8], P('cam', None, 'depth'), may hold values from 0 to 3
- frac_row: float32 [128, 4, 8], P('cam', None, 'depth'), may hold values from 0 to 1
- col_offset: int32 [128, 4, 8], P('cam', None, 'depth'), may hold values from -32 to 32
- frac_col: float32 [128, 4, 8], P('cam', None, 'depth'), may hold values from 0 to 1
- first_kernel: bfloat16 [8, 32, 3, 3, 3], replicated, may hold values from -0.21875 to 0.21875
- first_bias: float32 [8], replicated, may hold values from -0.5 to 0.5
- second_kernel: bfloat16 [8, 8, 3, 3, 3], replicated, may hold values from -0.4375 to 0.4375
- cotangent: bfloat16 [128, 8, 8, 4, 512], P('cam', None, 'depth'), may hold values from -6 to 6
Outputs:
- feature_grad: float32 [128, 32, 8, 512], P('cam', 'depth')
- first_grad: float32 [8, 32, 3, 3, 3], replicated
- second_grad: float32 [8, 8, 3, 3, 3], replicated
The draws below stay inside these ranges and needn't reach their ends.
All inputs are finite; a program needn't handle non-finite values. No bound on the sum of `view_mask` on one device may be relied on, other than what follows from the above.
Results may differ from the reference program's by a relative error of at most 0.0053.
Values may be sent and summed in bfloat16 or wider, within the bound.
No kernel may reach another device: no remote copies, remote signals or barrier semaphores. Data moves between devices by JAX's collectives and lax.ppermute only.
A program may use at most 128 MiB of HBM per device.

```python
import jax
import jax.numpy as jnp
from jax import lax

C = 32
K = 8
W = 512
D = 8
H = 4
SPAN = 4
SHIFT = 32
HS = 8
NCAM = 128


def set_ends(array, rng, smallest, high):
    spot = [jax.random.randint(jax.random.fold_in(rng, axis), (), 0, length) for axis, length in enumerate(array.shape)]
    widest = array.shape.index(max(array.shape))
    neighbour = spot[:widest] + [(spot[widest] + 1) % array.shape[widest]] + spot[widest + 1:]
    return array.at[tuple(spot)].set(smallest).at[tuple(neighbour)].set(high)


def steps_of(rng, shape, pieces, low, top_value):
    level = 1.0
    for dim, shards_of in pieces:
        draws = jax.random.uniform(jax.random.fold_in(jax.random.fold_in(rng, 6), dim), (shards_of,), jnp.float32, low / len(pieces), top_value / len(pieces))
        level = level * jnp.repeat(jnp.exp(draws), shape[dim] // shards_of).reshape((-1,) + (1,) * (len(shape) - 1 - dim))
    return level


def scatter_about(stream_key, dims, width, reach, shards=(), kind=jnp.bfloat16):
    gain = steps_of(stream_key, dims, shards, -0.22, 0.18) if shards else 1.0
    result = jax.random.normal(stream_key, dims, jnp.float32) * width * gain
    return jnp.minimum(jnp.maximum(result, -reach), reach).astype(kind)


def setup_inputs(seed: int = 0) -> dict:
    key_list = jax.random.split(jax.random.key(seed), 11)
    return {
        "features": scatter_about(key_list[0], (NCAM, C, HS, W), 1.0, 6.0, ((0, 128),)),
        "view_mask": set_ends((jax.random.randint(key_list[1], (NCAM, 4), 0, 4) < 3).astype(jnp.int32), jax.random.fold_in(key_list[1], 1), 0, 1),
        "row_offset": set_ends(jax.random.randint(key_list[2], (NCAM, 4, D), 0, SPAN), jax.random.fold_in(key_list[2], 1), 0, SPAN - 1).astype(jnp.int32),
        "frac_row": jnp.clip(1.0 * jax.random.uniform(key_list[3], (NCAM, 4, D), jnp.float32) ** steps_of(key_list[3], (NCAM, 4, D), ((0, 128), (2, 2)), -0.2, 0.2), 0.0, 1.0),
        "col_offset": set_ends(jax.random.randint(key_list[4], (NCAM, 4, D), -SHIFT, SHIFT + 1), jax.random.fold_in(key_list[4], 1), -SHIFT, SHIFT).astype(jnp.int32),
        "frac_col": jnp.clip(1.0 * jax.random.uniform(key_list[5], (NCAM, 4, D), jnp.float32) ** steps_of(key_list[5], (NCAM, 4, D), ((0, 128), (2, 2)), -0.2, 0.2), 0.0, 1.0),
        "first_kernel": scatter_about(key_list[6], (K, C, 3, 3, 3), (27 * C) ** -0.5, 0.21875),
        "first_bias": jnp.clip(jax.random.uniform(key_list[7], (K,), jnp.float32, -0.5, 0.5), -0.5, 0.5),
        "second_kernel": scatter_about(key_list[8], (K, K, 3, 3, 3), (27 * K) ** -0.5, 0.4375),
        "cotangent": scatter_about(key_list[9], (NCAM, K, D, H, W), 1.0, 6.0, ((0, 128), (2, 2))),
    }


view_offsets = (-2, -1, 1, 2)

def conv_same(volume, kernel, depth_pad):
    return lax.conv_general_dilated(volume[None], kernel, (1, 1, 1), [depth_pad, (1, 1), (1, 1)], dimension_numbers=('NCDHW', 'OIDHW', 'NCDHW'), preferred_element_type=jnp.float32)[0]

def flipped(kernel):
    return jnp.transpose(jnp.flip(kernel, (2, 3, 4)), (1, 0, 2, 3, 4))

def silu_slope(value):
    gate = jax.nn.sigmoid(value)
    return gate * (1.0 + value * (1.0 - gate))

def pad_source(src_band):
    return jnp.pad(src_band.astype(jnp.float32), ((0, 0), (0, 0), (SHIFT, SHIFT + 1)))

def plane_warp(padded, row_start, col_start, frac_r, frac_c):
    window = lax.dynamic_slice(padded, (jnp.zeros((), jnp.int32), row_start.astype(jnp.int32), (col_start + SHIFT).astype(jnp.int32)), (padded.shape[0], H + 1, W + 1))
    row_mixed = (1.0 - frac_r) * window[:, :H, :] + frac_r * window[:, 1:, :]
    return (1.0 - frac_c) * row_mixed[:, :, :W] + frac_c * row_mixed[:, :, 1:]

def slot_warp(padded, row_starts, col_starts, fracs_r, fracs_c):
    return jax.vmap(plane_warp, in_axes=(None, 0, 0, 0, 0), out_axes=1)(padded, row_starts, col_starts, fracs_r, fracs_c)

def weight_term(volume, grad_out):
    widened = volume.astype(jnp.float32)

    def convolve(kernel):
        return lax.conv_general_dilated(widened[None], kernel, (1, 1, 1), [(1, 1), (1, 1), (1, 1)], dimension_numbers=('NCDHW', 'OIDHW', 'NCDHW'), precision=lax.Precision.HIGHEST)[0]
    start_kernel = jnp.zeros((grad_out.shape[0], volume.shape[0], 3, 3, 3), jnp.float32)
    outcome, pullback = jax.vjp(convolve, start_kernel)
    return pullback(grad_out.astype(jnp.float32))[0]

def reference(features, view_mask, row_offset, frac_row, col_offset, frac_col, first_kernel, first_bias, second_kernel, cotangent):
    top_row = SPAN // 2

    def per_camera(carried, camera):
        grad_total, grad_first, grad_second = carried
        own_band = features[camera]
        reference_view = own_band[:, top_row:top_row + H, :].astype(jnp.float32)[:, None]
        view_weights = view_mask[camera].astype(jnp.float32)
        view_count = 1.0 + jnp.sum(view_weights)
        first_moment = reference_view
        second_moment = reference_view * reference_view
        paddings, warps, owners = ([], [], [])
        for slot_id in range(4):
            owner = (camera + view_offsets[slot_id]) % NCAM
            padded = pad_source(features[owner])
            warped = slot_warp(padded, row_offset[camera, slot_id], col_offset[camera, slot_id], frac_row[camera, slot_id], frac_col[camera, slot_id])
            first_moment = first_moment + view_weights[slot_id] * warped
            second_moment = second_moment + view_weights[slot_id] * (warped * warped)
            paddings.append(padded)
            warps.append(warped)
            owners.append(owner)
        view_mean = first_moment / view_count
        cost_volume = (second_moment / view_count - view_mean * view_mean).astype(jnp.bfloat16)
        pre_act = conv_same(cost_volume, first_kernel, (1, 1)) + first_bias[:, None, None, None]
        hidden = jax.nn.silu(pre_act).astype(jnp.bfloat16)
        cot_camera = cotangent[camera]
        hidden_grad = conv_same(cot_camera, flipped(second_kernel), (1, 1))
        pre_grad = (hidden_grad * silu_slope(pre_act)).astype(jnp.bfloat16)
        cost_grad = conv_same(pre_grad, flipped(first_kernel), (1, 1))
        grad_first = grad_first + weight_term(cost_volume, pre_grad)
        grad_second = grad_second + weight_term(hidden, cot_camera)
        scaled = 2.0 * cost_grad / view_count
        ref_grad = lax.optimization_barrier(jnp.sum(scaled * (reference_view - view_mean), axis=1))
        grad_total = grad_total.at[camera].add(jnp.pad(ref_grad, ((0, 0), (top_row, SPAN - top_row), (0, 0))))
        for slot_id in range(4):
            slot_grad = view_weights[slot_id] * scaled * (warps[slot_id] - view_mean)
            outcome, pullback = jax.vjp(lambda padded_src: slot_warp(padded_src, row_offset[camera, slot_id], col_offset[camera, slot_id], frac_row[camera, slot_id], frac_col[camera, slot_id]), paddings[slot_id])
            source_grad = pullback(slot_grad)[0][:, :, SHIFT:SHIFT + W]
            grad_total = grad_total.at[owners[slot_id]].add(source_grad)
        return ((grad_total, grad_first, grad_second), None)
    initial = (jnp.zeros(features.shape, jnp.float32), jnp.zeros(first_kernel.shape, jnp.float32), jnp.zeros(second_kernel.shape, jnp.float32))
    finals, outcome = lax.scan(per_camera, initial, jnp.arange(NCAM, dtype=jnp.int32))
    grad_scale = (NCAM * D * H * W) ** (-0.5)
    return (finals[0], finals[1] * grad_scale, finals[2] * grad_scale)
```

```python
import jax
import jax.numpy as jnp
from jax import lax
from jax.experimental import pallas as pl
from jax.experimental.pallas import tpu as pltpu
from jax.sharding import PartitionSpec as P

W = 512
D = 8
H = 4
C = 32
K = 8
HS = 8
SPAN = 4
SHIFT = 32
HALF = C // 2
WP = W + 128
LANES = 128

view_offsets = (-2, -1, 1, 2)
CAM_STEPS = ((1, 2, 3), (4, 12, 8), (16, 32, 48), (96,))


f32 = jnp.float32
bf16 = jnp.bfloat16


def from_behind(x, axis, by):
    size = lax.axis_size(axis)
    return lax.ppermute(x, axis, [(i, (i + by) % size) for i in range(size)])


def partner(x):
    size = lax.axis_size("cam")
    return lax.ppermute(x, "cam", [(i, i ^ 1) for i in range(size)])


def across(x):
    size = lax.axis_size("cam")
    return lax.ppermute(x, "cam", [(i, (i + (2 * (i % 2) - 1)) % size) for i in range(size)])


def dot_nn(a, b):
    return lax.dot_general(a, b, (((1,), (0,)), ((), ())), preferred_element_type=f32)


def dot_nt(a, b):
    return lax.dot_general(a, b, (((1,), (1,)), ((), ())), preferred_element_type=f32)


def lane_iota(shape):
    return lax.broadcasted_iota(jnp.int32, shape, 1)


def to_right(x):
    return jnp.where(lane_iota(x.shape) == 0, 0.0, pltpu.roll(x, 1, 1))


def to_left(x):
    return jnp.where(lane_iota(x.shape) == x.shape[1] - 1, 0.0, pltpu.roll(x, x.shape[1] - 1, 1))


def three_taps(x):
    left, right = to_left(x), to_right(x)
    parts = []
    for h in range(H):
        for y in (left, x, right):
            parts.append(y[h * K : (h + 1) * K])
    return jnp.concatenate(parts, axis=0)


def chunks_of(x):
    return [x[:, i * LANES : (i + 1) * LANES] for i in range(x.shape[1] // LANES)]


def pull_lanes(x, shift, keep):
    blocks = chunks_of(x)
    turn = (LANES - shift) & (LANES - 1)
    return jnp.concatenate(
        [pltpu.roll(jnp.where(keep, a, b), turn, 1) for a, b in zip(blocks[:-1], blocks[1:])],
        axis=1,
    )


def push_lanes(x, shift, keep):
    rolled = [pltpu.roll(y, shift, 1) for y in chunks_of(x)]
    zero = jnp.zeros_like(rolled[0])
    return jnp.concatenate(
        [jnp.where(keep, a, b) for a, b in zip(rolled + [zero], [zero] + rolled)], axis=1
    )


def put_rows(ref, start, x):
    for i, y in enumerate(chunks_of(x)):
        ref[i, pl.ds(start, x.shape[0]), :] = y


def strided_rows(ref, start, count, stride):
    return jnp.concatenate(
        [ref[i, pl.ds(start, count, stride=stride), :] for i in range(W // LANES)], axis=1
    )


def banded(block_of, width, kd):
    rows = []
    for h in range(H):
        for kw in range(3):
            pieces = []
            for row in range(H):
                kh = row - h + 1
                if 0 <= kh <= 2:
                    pieces.append(block_of(kd, kh, kw))
                else:
                    pieces.append(jnp.zeros((K, width), f32))
            if width * H < LANES:
                pieces.append(jnp.zeros((K, LANES - width * H), f32))
            rows.append(jnp.concatenate(pieces, axis=1))
    return jnp.concatenate(rows, axis=0)


def main_kernel(
    where_ref,
    par_own,
    par_peer,
    mask_ref,
    bias_ref,
    own_ref,
    n0_ref,
    n1_ref,
    n2_ref,
    n3_ref,
    k1_ref,
    k2_ref,
    cot_own,
    cot_peer,
    weight_out,
    own_out,
    s0_out,
    s1_out,
    s2_out,
    s3_out,
    flat,
    bands,
    refs,
    cot_flat,
    a1,
    a1t,
    a2t,
    cot3,
    pre3,
    costs,
    hids,
    warps,
    means,
    own_acc,
    acc,
):
    dep = where_ref[0]
    half = pl.multiple_of(dep * HALF, HALF)

    for kd in range(3):
        m1 = banded(lambda d, h, w: k1_ref[d, h, w].astype(f32), C, kd)
        a1[:, kd * LANES : (kd + 1) * LANES] = m1.astype(bf16)
        a1t[kd] = m1.T.astype(bf16).reshape(H, C, 96)
        m2 = banded(lambda d, h, w: k2_ref[d, h, w].astype(f32), K, kd)
        a2t[kd] = m2.T[: H * K].astype(bf16)

    for buf in (cot3, pre3, costs, hids):
        zero = jnp.zeros(buf.shape[1:], bf16)
        buf[0] = zero
        buf[D + 1] = zero

    for side, cot in enumerate((cot_own, cot_peer)):
        put_rows(cot_flat, 0, cot[: K * 16, :].astype(f32))
        first_plane = (dep if side == 0 else 1 - dep) * (D // 2)
        for d in range(D // 2):
            x = jnp.concatenate(
                [strided_rows(cot_flat, d * H + h, K, 16) for h in range(H)], axis=0
            )
            cot3[first_plane + d + 1] = three_taps(x).astype(bf16)

    put_rows(flat, 0, own_ref[...].astype(f32).reshape(C * HS, W))
    for h in range(H):
        refs[h] = strided_rows(flat, SPAN // 2 + h, C, HS)
    odd = where_ref[1]
    roles = (1 - odd + 1, 1 + odd, 3 * odd, 3 - 3 * odd)
    for s, n_ref in zip(roles, (n0_ref, n1_ref, n2_ref, n3_ref)):
        put_rows(flat, 0, n_ref[...].astype(f32).reshape(C * HS, W))
        for r in range(HS):
            x = strided_rows(flat, r, C, HS)
            x = jnp.concatenate([x, jnp.zeros((C, LANES), f32)], axis=1)
            bands[s, r] = pltpu.roll(x, SHIFT, 1)

    weights = [mask_ref[0, s].astype(f32) for s in range(4)]
    inverse = 1.0 / (jnp.full((1, W), 1.0, f32) + weights[0] + weights[1] + weights[2] + weights[3])
    lanes = lane_iota((HALF, LANES))

    def parameters(d):
        mine = (d // (D // 2)) == dep
        local = d % (D // 2)

        def pick(row):
            return jnp.where(mine, par_own[row, local], par_peer[row, local])

        return [
            (
                pick(s).astype(jnp.int32),
                pick(4 + s).astype(jnp.int32) + SHIFT,
                pick(8 + s),
                pick(12 + s),
            )
            for s in range(4)
        ]

    @pl.loop(0, D)
    def _(d):
        slots = parameters(d)
        keeps = [(lanes >= c, lanes >= c + 1) for _, c, _, _ in slots]
        for part in range(2):
            off = pl.multiple_of(((dep + part) % 2) * HALF, HALF)
            for h in range(H):
                view = refs[h, pl.ds(off, HALF), :]
                first = view
                second = view * view
                for s, (r, c, fr, fc) in enumerate(slots):
                    mixed = (1.0 - fr) * bands[s, r + h, pl.ds(off, HALF), :] + fr * bands[
                        s, r + h + 1, pl.ds(off, HALF), :
                    ]
                    warped = (weights[s] * (1.0 - fc)) * pull_lanes(mixed, c, keeps[s][0]) + (
                        weights[s] * fc
                    ) * pull_lanes(mixed, c + 1, keeps[s][1])
                    if part == 0:
                        warps[s, d, h] = warped
                    first = first + warped
                    second = second + warped * warped
                mean = first * inverse
                if part == 0:
                    means[d, h] = mean
                cost = second * inverse - mean * mean
                costs[d + 1, pl.ds(pl.multiple_of(h * C + off, HALF), HALF), :] = cost.astype(bf16)

    rows = lax.broadcasted_iota(jnp.int32, (H * K, W), 0) % K
    bias = jnp.zeros((H * K, W), f32)
    for o in range(K):
        bias = jnp.where(rows == o, bias_ref[o], bias)

    @pl.loop(0, D, unroll=4)
    def _(d):
        y = dot_nn(a1[...], costs[pl.ds(d, 3)].reshape(3 * H * C, W))
        taps = [
            jnp.concatenate([y[h * 24 + kw * K : h * 24 + (kw + 1) * K] for h in range(H)], axis=0)
            for kw in range(3)
        ]
        pre = taps[1] + to_right(taps[0]) + to_left(taps[2]) + bias
        gate = jax.nn.sigmoid(pre)
        hids[d + 1] = (pre * gate).astype(bf16)
        grad = dot_nn(a2t[0], cot3[d + 2]) + dot_nn(a2t[1], cot3[d + 1]) + dot_nn(a2t[2], cot3[d])
        grad = grad * (gate * (1.0 + pre * (1.0 - gate)))
        pre3[d + 1] = three_taps(grad).astype(bf16)

    g1 = jnp.zeros((96, 3 * LANES), f32)
    g2 = jnp.zeros((96, 96), f32)
    for d in range(D):
        g1 = g1 + dot_nt(pre3[d + 1], costs[pl.ds(d, 3)].reshape(3 * H * C, W))
        g2 = g2 + dot_nt(cot3[d + 1], hids[pl.ds(d, 3)].reshape(3 * H * K, W))
    g2 = jnp.concatenate([g2, jnp.zeros((96, LANES - 96), f32)], axis=1)
    lanes24 = lane_iota((24, LANES))
    for kd in range(3):
        total = jnp.zeros((24, LANES), f32)
        for h in range(H):
            block = g1[h * 24 : (h + 1) * 24, kd * LANES : (kd + 1) * LANES]
            block = pltpu.roll(block, ((1 - h) * C) % LANES, 1) if h != 1 else block
            low, high = (C if h == 0 else 0), (2 * C if h == H - 1 else 3 * C)
            total = total + jnp.where((lanes24 >= low) & (lanes24 < high), block, 0.0)
            block = pltpu.roll(
                g2[h * 24 : (h + 1) * 24], (96 - kd * H * K - (h - 1) * K) % LANES, 1
            )
            low, high = 96 + (K if h == 0 else 0), 96 + (2 * K if h == H - 1 else 3 * K)
            total = total + jnp.where((lanes24 >= low) & (lanes24 < high), block, 0.0)
        weight_out[kd * 24 : (kd + 1) * 24, :] = total

    acc[...] = jnp.zeros(acc.shape, f32)
    own_acc[...] = jnp.zeros(own_acc.shape, f32)

    @pl.loop(0, D)
    def _(d):
        slots = parameters(d)
        keeps = [(lanes >= c, lanes >= c + 1) for _, c, _, _ in slots]

        def kernel_part(kd):
            return a1t[kd, :, pl.ds(half, HALF), :].reshape(H * HALF, 96)

        grad = (
            dot_nn(kernel_part(0), pre3[d + 2])
            + dot_nn(kernel_part(1), pre3[d + 1])
            + dot_nn(kernel_part(2), pre3[d])
        )
        scaled = grad * (2.0 * inverse)
        for h in range(H):
            own_acc[h] = own_acc[h] + scaled[h * HALF : (h + 1) * HALF] * (
                refs[h, pl.ds(half, HALF), :] - means[d, h]
            )
        for s, (r, c, fr, fc) in enumerate(slots):
            carried = None
            for h in range(H):
                slot = scaled[h * HALF : (h + 1) * HALF] * (warps[s, d, h] - means[d, h])
                mixed = (weights[s] * (1.0 - fc)) * push_lanes(slot, c, keeps[s][0]) + (
                    weights[s] * fc
                ) * push_lanes(slot, c + 1, keeps[s][1])
                lower = (1.0 - fr) * mixed
                if carried is not None:
                    lower = lower + carried
                acc[s, r + h] = acc[s, r + h] + lower
                carried = fr * mixed
            acc[s, r + H] = acc[s, r + H] + carried

    def gather_rows(row_of):
        for r in range(HS):
            x = row_of(r)
            for i, y in enumerate(chunks_of(x)):
                flat[i, pl.ds(r, HALF, stride=HS), :] = y
        return jnp.concatenate([flat[i, : HALF * HS, :] for i in range(W // LANES)], axis=1)

    top = SPAN // 2
    own_out[...] = gather_rows(
        lambda r: own_acc[r - top] if top <= r < top + H else jnp.zeros((HALF, W), f32)
    )
    for s, out in zip(roles, (s0_out, s1_out, s2_out, s3_out)):
        out[...] = gather_rows(lambda r: pltpu.roll(acc[s, r], WP - SHIFT, 1)[:, :W]).astype(bf16)


def run_main(where, par_own, par_peer, mask, bias, own, near, k1, k2, cot_own, cot_peer):
    smem = pl.BlockSpec(memory_space=pltpu.SMEM)
    vmem = pl.BlockSpec(memory_space=pltpu.VMEM)
    return pl.pallas_call(
        main_kernel,
        out_shape=(
            jax.ShapeDtypeStruct((72, LANES), f32),
            jax.ShapeDtypeStruct((HALF * HS, W), f32),
        )
        + (jax.ShapeDtypeStruct((HALF * HS, W), bf16),) * 4,
        in_specs=[smem] * 5 + [vmem] * 9,
        out_specs=(vmem,) * 6,
        scratch_shapes=[
            pltpu.VMEM((W // LANES, C * HS, LANES), f32),
            pltpu.VMEM((4, HS, C, WP), f32),
            pltpu.VMEM((H, C, W), f32),
            pltpu.VMEM((W // LANES, K * 16, LANES), f32),
            pltpu.VMEM((96, 3 * LANES), bf16),
            pltpu.VMEM((3, H, C, 96), bf16),
            pltpu.VMEM((3, H * K, 96), bf16),
            pltpu.VMEM((D + 2, 96, W), bf16),
            pltpu.VMEM((D + 2, 96, W), bf16),
            pltpu.VMEM((D + 2, H * C, W), bf16),
            pltpu.VMEM((D + 2, H * K, W), bf16),
            pltpu.VMEM((4, D, H, HALF, W), f32),
            pltpu.VMEM((D, H, HALF, W), f32),
            pltpu.VMEM((H, HALF, W), f32),
            pltpu.VMEM((4, HS, HALF, WP), f32),
        ],
        cost_estimate=pl.CostEstimate(flops=2_000_000_000, bytes_accessed=4_000_000, transcendentals=0),
        name="main",
    )(where, par_own, par_peer, mask, bias, own, *near, k1, k2, cot_own, cot_peer)


def finish_kernel(*refs):
    *parts, first, second = refs
    cams = 2**7
    total = parts[0][...]
    for part in parts[1:]:
        total = total + part[...]
    total = total * ((cams * D * H * W) ** (-0.5))
    for kd in range(3):
        for kw in range(3):
            block = total[kd * 24 + kw * K : kd * 24 + (kw + 1) * K]
            for kh in range(3):
                first[kd, kh, kw] = block[:, kh * C : (kh + 1) * C]
                second[kd, kh, kw] = block[:, 96 + kh * K : 96 + (kh + 1) * K]


def finish(parts):
    vmem = pl.BlockSpec(memory_space=pltpu.VMEM)
    return pl.pallas_call(
        finish_kernel,
        out_shape=(
            jax.ShapeDtypeStruct((3, 3, 3, K, C), f32),
            jax.ShapeDtypeStruct((3, 3, 3, K, K), f32),
        ),
        in_specs=[vmem] * len(parts),
        out_specs=(vmem, vmem),
        name="finish",
    )(*parts)


def exchanged(x, steps):
    size = lax.axis_size("cam")
    return [lax.ppermute(x, "cam", [(i, i ^ step) for i in range(size)]) for step in steps]


def shards(
    features,
    view_mask,
    row_offset,
    frac_row,
    col_offset,
    frac_col,
    first_kernel,
    first_bias,
    second_kernel,
    cotangent,
):
    own = features[0]
    beside = partner(own)
    near = across(own)
    far = across(beside)
    next_near = partner(near)
    par_own = jnp.concatenate(
        [row_offset[0].astype(f32), col_offset[0].astype(f32), frac_row[0], frac_col[0]], axis=0
    )
    cot_own = cotangent[0]
    rest = par_own.reshape(1, 64)
    terms = []
    for _ in range(3):
        term = lax.reduce_precision(rest, 8, 7)
        terms.append(term.astype(bf16))
        rest = rest - term
    row = jnp.concatenate(terms + [jnp.zeros((1, W - 192), bf16)], axis=1)
    sent = jnp.concatenate([cot_own.reshape(K * 16, W), jnp.pad(row, ((0, 15), (0, 0)))], axis=0)
    got = from_behind(sent, "depth", 1)
    cot_peer = got[: K * 16]
    row = got[K * 16, :192].astype(f32).reshape(3, 16, 4)
    par_peer = row[0] + (row[1] + row[2])
    where = jnp.stack([lax.axis_index("depth"), lax.axis_index("cam") % 2]).astype(jnp.int32)
    weight_part, own_part, *parts = run_main(
        where,
        par_own,
        par_peer,
        view_mask,
        first_bias,
        own,
        (beside, near, far, next_near),
        jnp.transpose(first_kernel, (2, 3, 4, 0, 1)),
        jnp.transpose(second_kernel, (2, 3, 4, 0, 1)),
        sent,
        got,
    )
    for_beside, for_near, for_far, for_next = parts

    def added(*terms):
        return sum((term.astype(f32) for term in terms[1:]), terms[0].astype(f32))

    sums = weight_part
    for stage, steps in enumerate(CAM_STEPS):
        pieces = [sums] + exchanged(sums, steps)
        if stage == 0:
            handed = partner(for_next)
            far_back = across(for_far)
        elif stage == 1:
            near_back = across(added(for_near, handed).astype(bf16))
        elif stage == 2:
            beside_back = partner(added(for_beside, far_back).astype(bf16))
        if stage < len(CAM_STEPS) - 1:
            sums = sum(pieces[1:], pieces[0])
            if stage == 0:
                handed, sums = lax.optimization_barrier((handed, sums))
            elif stage == 1:
                far_back, sums = lax.optimization_barrier((far_back, sums))
    total = added(own_part, near_back, beside_back)
    first, second = finish(pieces)
    return (
        total.reshape(1, HALF, HS, W),
        jnp.transpose(first, (3, 4, 0, 1, 2)),
        jnp.transpose(second, (3, 4, 0, 1, 2)),
    )


def solution(mesh):
    placed = (
        P("cam", None, None, None),
        P("cam", None),
        P("cam", None, "depth"),
        P("cam", None, "depth"),
        P("cam", None, "depth"),
        P("cam", None, "depth"),
        P(),
        P(),
        P(),
        P("cam", None, "depth", None, None),
    )
    return jax.shard_map(
        shards,
        mesh=mesh,
        in_specs=placed,
        out_specs=(P("cam", "depth", None, None), P(), P()),
        check_vma=False,
    )
```
